32 devices in a mesh: groups: 2 (over y), space: 8 (over z, core), tm: 2 (over x), rep: 1.
Axes of the slice: x: 2, y: 2, z: 4, core: 2. Of those that a mesh axis runs over, the one named last changes fastest.
Arguments:
- noise: float32 [8192, 4096], P(('groups', 'space'), 'tm'), parts along dimension 0, may hold values from -6 to 6
- factor: float32 [4096, 4096], P(('tm', 'rep'), 'space'), may hold values from -8 to 8, as said below
- col_blocks: int32 [64, 4], P(('groups', 'space')), parts along dimension 0, may hold values from 0 to 31, as said below
- block_values: float32 [64, 4, 128, 128], P(('groups', 'space')), parts along dimension 0, may hold values from -0.25 to 0.25
Outputs:
- samples: float32 [8192, 4096], P(('groups', 'space'), ('tm', 'rep')), parts along dimension 0
The draws below stay inside these ranges and needn't reach their ends.
There are 2 independent parts, one for each index of `groups`. The reference program is written for one: setup_inputs(seed, part) draws one part's arguments, and reference() takes and returns one part's arrays. A program takes and returns all parts, laid end to end along the dimension named above; an argument that names none is the same for every part. Nothing has to cross between parts.
Inputs may be any that keep to these rules, and one draw needn't show every extreme that they name: factor is lower triangular: every entry above the diagonal is zero, and the diagonal lies in 0.5 to 1.5. `col_blocks`: in every row b the first entry is b itself; the other 3 entries are distinct blocks whose circular distance from b (modulo 32) is 1 to 2.
All inputs are finite; a program needn't handle non-finite values.
Results may differ from the reference program's by a relative error of at most 0.0003.
Values sent between devices are 32-bit elements; how exact they have to be, the bound alone decides.
No kernel may reach another device: no remote copies, remote signals or barrier semaphores. Data moves between devices by JAX's collectives and lax.ppermute only.
A program may use at most 128 MiB of HBM per device.

```python
import jax
import jax.numpy as jnp
from jax import lax

BS = 128
REACH = 2
HOURS = 4096
K = 4
NBLOCKS = 32
NODES = 4096


def draw_factor(key, part):
    first_key, second_key = jax.random.split(key, 2)
    rows = jnp.arange(HOURS)[:, None]
    cols = jnp.arange(HOURS)[None, :]
    entries = jnp.clip(jax.random.normal(first_key, (HOURS, HOURS), jnp.float32), -6.0, 6.0)
    scaled = entries / jnp.sqrt(rows.astype(jnp.float32) + 1.0)
    lower = jnp.where(cols < rows, scaled, 0.0)
    diagonal = jax.random.uniform(second_key, (HOURS,), jnp.float32, 0.5, 1.5)
    return (lower + jnp.diag(diagonal)).astype(jnp.float32)


def draw_col_blocks(key, part):
    base = jnp.arange(2 * REACH)
    offsets = base - REACH + (base >= REACH).astype(jnp.int32)
    scores = jax.random.randint(key, (NBLOCKS, 2 * REACH), 0, 1 << 20) * (2 * REACH) + base[None, :]
    order = jnp.argsort(scores, axis=1)[:, :K - 1]
    picked = offsets[order]
    own = jnp.arange(NBLOCKS)[:, None]
    others = (own + picked) % NBLOCKS
    return jnp.concatenate([own, others], axis=1).astype(jnp.int32)


def block_scale(key, shape, cuts, smallest, high):
    factor_of, own = 1.0, jax.random.fold_in(key, 6)
    for position, blocks in cuts:
        draws = jnp.exp(jax.random.uniform(jax.random.fold_in(own, position), (blocks,), jnp.float32, smallest / len(cuts), high / len(cuts)))
        factor_of = factor_of * jnp.repeat(draws, shape[position] // blocks).reshape([-1 if axis == position else 1 for axis in range(len(shape))])
    return factor_of


def centred(key, shape, scale, most, shards=(), dtype=jnp.bfloat16):
    array = jax.random.normal(key, shape, jnp.float32) * scale
    if len(shards) > 0:
        array = block_scale(key, shape, shards, -0.22, 0.18) * array
    return jnp.clip(array, min=-most, max=most).astype(dtype)


def setup_inputs(seed: int = 0, part: int = 0) -> dict:
    keys = jax.random.split(jax.random.key(seed), 5)
    part_splits = jax.random.split(jax.random.fold_in(keys[4], part), 5)
    noise = centred(part_splits[0], (NODES, HOURS), 1.0, 6.0, ((0, 8), (1, 2)), jnp.float32)
    factor = draw_factor(jax.random.fold_in(keys[4], 71), part)
    col_blocks = draw_col_blocks(jax.random.fold_in(jax.random.fold_in(keys[4], part), 71), part)
    block_values = centred(part_splits[3], (NBLOCKS, K, BS, BS), (K * BS) ** -0.5, 0.25, ((0, 8),), jnp.float32)
    return {"noise": noise, "factor": factor, "col_blocks": col_blocks, "block_values": block_values}


def reference(noise, factor, col_blocks, block_values):
    colored = jnp.dot(noise, factor.T, precision=lax.Precision.HIGHEST, preferred_element_type=jnp.float32)
    blocks = colored.reshape(NBLOCKS, BS, HOURS)

    def block_row(operands):
        columns, values = operands
        picked = blocks[columns.astype(jnp.int32)]
        return jnp.einsum("kab,kbh->ah", values.astype(jnp.float32), picked, precision=lax.Precision.HIGHEST)

    result = lax.map(block_row, (col_blocks, block_values))
    return result.reshape(NODES, HOURS)
```

```python
import functools

import jax
import jax.numpy as jnp
from jax import lax
from jax.experimental import pallas as pl
from jax.experimental.pallas import tpu as pltpu
from jax.sharding import PartitionSpec as P

BS = 128
REACH = 2
F32 = jnp.float32
BF16 = jnp.bfloat16
ANY = pl.BlockSpec(memory_space=pl.ANY)
VMEM = pl.BlockSpec(memory_space=pltpu.VMEM)
SMEM = pl.BlockSpec(memory_space=pltpu.SMEM)
NT = (((1,), (1,)), ((), ()))
NN = (((1,), (0,)), ((), ()))


def shifted(block, axis, distance):
    devices = range(lax.axis_size(axis))
    route = [(i - distance, i) for i in devices if i - distance in devices]
    return lax.ppermute(block, axis, route)


def extended_2(block, sides, width):
    for axis, dim in sides:
        count = lax.axis_size(axis)
        forward = [(i, i + 1) for i in range(count - 1)]
        forward.append((count - 1, 0))
        backward = [(target, source) for source, target in forward]
        low = lax.ppermute(
            lax.slice_in_dim(block, block.shape[dim] - width, None, axis=dim), axis, forward
        )
        high = lax.ppermute(lax.slice_in_dim(block, 0, width, axis=dim), axis, backward)
        block = jnp.concatenate([low, block, high], axis=dim)
    return block


def general(noise, factor, col_blocks, block_values):
    node_rows = noise.shape[0]
    hour_cols = noise.shape[1]
    tm_index = lax.axis_index("tm")
    tm_count = lax.axis_size("tm")
    every_hour = jnp.zeros((node_rows, hour_cols * tm_count), F32)
    every_hour = lax.dynamic_update_slice_in_dim(every_hour, noise, tm_index * hour_cols, 1)
    moving = noise
    for step in range(1, tm_count):
        moving = shifted(moving, "tm", 1)
        slot = jnp.maximum(tm_index - step, 0) * hour_cols
        placed = lax.dynamic_update_slice_in_dim(every_hour, moving, slot, 1)
        every_hour = jnp.where(tm_index >= step, placed, every_hour)
    colored = lax.dot_general(
        every_hour,
        lax.all_gather(factor, "space", axis=1, tiled=True),
        (((1,), (1,)), ((), ())),
        precision=lax.Precision.HIGHEST,
        preferred_element_type=F32,
    )
    extended = extended_2(colored, (("space", 0),), REACH * BS)
    local_blocks = node_rows // BS
    out_cols = colored.shape[1]
    ext_blocks = extended.reshape(local_blocks + 2 * REACH, BS, out_cols)
    all_blocks = lax.axis_size("space") * local_blocks
    local_rows = jnp.arange(local_blocks, dtype=jnp.int32)[:, None]
    global_rows = lax.axis_index("space") * local_blocks + local_rows
    offsets = (col_blocks - global_rows + REACH) % all_blocks - REACH
    positions = local_rows + REACH + offsets
    picked = ext_blocks[positions]
    result = jnp.einsum("nkab,nkbh->nah", block_values, picked, precision=lax.Precision.HIGHEST)
    return result.reshape(node_rows, out_cols)


def split(value):
    high = value.astype(BF16)
    return high, (value - high.astype(F32)).astype(BF16)


def precision_kernel(side, scal, cols, values, own_keep, own_send, far_keep, far_send, keep, send, hi, lo):
    core, first, total = scal[3], scal[5], scal[6]
    half = far_keep.shape[0]
    for own, far, out in ((own_keep, far_keep, keep), (own_send, far_send, send)):
        own_at = 0 if side == "mid" else half
        far_at = 2 * half if side == "mid" else 0
        for part in range(2):
            at = own_at + jnp.where(core == 0, part, 1 - part) * half
            at = pl.multiple_of(at, half)
            high, low = split(own[part * half : (part + 1) * half, :])
            hi[pl.ds(at, half), :] = high
            lo[pl.ds(at, half), :] = low
        high, low = split(far[...])
        hi[far_at : far_at + half, :] = high
        lo[far_at : far_at + half, :] = low
        rows = half // BS
        for i in range(rows):
            mid_rows = core == 0 if side == "mid" else core == 1
            row = i + jnp.where(mid_rows, rows, 0)
            picked_hi, picked_lo, left = [], [], []
            for k in range(values.shape[1]):
                offset = cols[row, k] - first - row
                offset = lax.rem(offset + REACH + 2 * total, total) - REACH
                place = row + REACH + offset
                group = place // REACH
                group = jnp.where(core == 0, group, 3 - group)
                group = group - (1 if side == "mid" else 0)
                group = jnp.clip(group, 0, 2)
                at = pl.multiple_of((group * REACH + lax.rem(place, REACH)) * BS, BS)
                picked_hi.append(hi[pl.ds(at, BS), :])
                picked_lo.append(lo[pl.ds(at, BS), :])
                left.append(values[i, k])
            left_hi, left_lo = split(jnp.concatenate(left, axis=1))
            right_hi = jnp.concatenate(picked_hi, axis=0)
            right_lo = jnp.concatenate(picked_lo, axis=0)
            acc = lax.dot_general(left_hi, right_hi, NN, preferred_element_type=F32)
            acc += lax.dot_general(left_lo, right_hi, NN, preferred_element_type=F32)
            acc += lax.dot_general(left_hi, right_lo, NN, preferred_element_type=F32)
            out[i * BS : (i + 1) * BS, :] = acc


def precision(side, scal, cols, values, own, far, tile):
    half, hours = far.shape
    nodes = own.shape[0]
    pairs = hours // (2 * tile)
    kept = lambda q, s, c: (0, 2 * q + s[3])
    sent = lambda q, s, c: (0, 2 * q + 1 - s[3])
    at = (lambda q, s, c: (1 - s[3], 0, 0, 0)) if side == "mid" else (lambda q, s, c: (s[3], 0, 0, 0))
    piece = jax.ShapeDtypeStruct((half, hours // 2), F32)
    return pl.pallas_call(
        functools.partial(precision_kernel, side),
        out_shape=(piece, piece),
        grid_spec=pltpu.PrefetchScalarGridSpec(
            num_scalar_prefetch=2,
            grid=(pairs,),
            in_specs=[
                pl.BlockSpec((half // BS,) + values.shape[1:], at),
                pl.BlockSpec((nodes, tile), kept),
                pl.BlockSpec((nodes, tile), sent),
                pl.BlockSpec((half, tile), kept),
                pl.BlockSpec((half, tile), sent),
            ],
            out_specs=[pl.BlockSpec((half, tile), lambda q, s, c: (0, q))] * 2,
            scratch_shapes=[pltpu.VMEM((3 * half, tile), BF16)] * 2,
        ),
        compiler_params=pltpu.CompilerParams(vmem_limit_bytes=24 << 20),
        cost_estimate=pl.CostEstimate(
            flops=6 * half * values.shape[1] * BS * hours, bytes_accessed=16 * half * hours, transcendentals=0
        ),
        name="precision_" + side,
    )(scal, cols, values, own, own, far, far)


def prepare_kernel(scal, mine, theirs, *refs):
    tile = mine.shape[1]
    for piece, out in ((mine, refs[-2]), (theirs, refs[-1])):
        high, low = split(piece[...])
        out[0, :, :tile] = high
        out[0, :, tile:] = low


def prepare(scal, mine, theirs, outer, received, before, tile):
    half, width = mine.shape
    tiles = width // tile

    def place(q, s):
        owner = 1 - s[1] if received else s[1]
        return (owner * tiles + q, outer, 0)

    whole = jax.ShapeDtypeStruct((2 * tiles, 2 * half, 2 * tile), BF16)
    return pl.pallas_call(
        prepare_kernel,
        out_shape=(whole, whole),
        grid_spec=pltpu.PrefetchScalarGridSpec(
            num_scalar_prefetch=1,
            grid=(tiles,),
            in_specs=[pl.BlockSpec((half, tile), lambda q, s: (0, q))] * 2 + [ANY] * len(before),
            out_specs=[pl.BlockSpec((1, half, 2 * tile), place)] * 2,
        ),
        input_output_aliases={3: 0, 4: 1} if before else {},
        compiler_params=pltpu.CompilerParams(vmem_limit_bytes=16 << 20),
        cost_estimate=pl.CostEstimate(flops=0, bytes_accessed=16 * half * width, transcendentals=0),
        name="prepare",
    )(scal, mine, theirs, *before)


def multiply_kernel(jobs, band, first, scal, mine, theirs, *refs):
    refs = list(refs)
    before = [] if first else [refs.pop(0), refs.pop(0)]
    count = 1 + max(source for source, _, _, _ in jobs)
    sources = [refs.pop(0) for _ in range(count)]
    acc_mine, acc_theirs, buf, both, low, sems = refs
    group, hour, chip, core = scal[0], scal[1], scal[2], scal[3]
    chips = scal[4]
    height, width = buf.shape[1:]
    nrows = acc_mine.shape[1]
    step = min(256, nrows)

    plan = []
    for n, (source, row, hop, kind) in enumerate(jobs):
        owner = chip + hop
        where = row if kind == "own" else group if kind == "direct" else 1 - group
        bottom = hour * (4 * height) + (2 * band + where + 1) * height
        valid = (owner >= 0) & (owner < chips) & ((2 * owner + core) * width < bottom)
        src = sources[source]
        if kind == "own":
            src = src.at[pl.ds((2 * band + row) * height, height), :]
        plan.append((valid, owner, where, pltpu.make_async_copy(src, buf.at[n], sems.at[n])))
    for valid, _, _, copy in plan:
        pl.when(valid)(copy.start)

    for r in range(acc_mine.shape[0]):
        for out, old in zip((acc_mine, acc_theirs), before or (None, None)):
            @pl.loop(0, nrows // step)
            def _(m):
                at = pl.ds(pl.multiple_of(m * step, step), step)
                out[r, at, :] = jnp.zeros((step, height), F32) if first else old[r, at, :]

    for n, (valid, owner, where, copy) in enumerate(plan):
        @pl.when(valid)
        def _():
            copy.wait()

            @pl.loop(0, height // 128)
            def _(m):
                at = pl.ds(pl.multiple_of(m * 128, 128), 128)
                hi, lo = split(buf[n, at, :])
                both[at, :width] = hi
                both[at, width:] = hi
                low[at, :] = lo

            for out, left in ((acc_theirs, theirs), (acc_mine, mine)):
                @pl.loop(0, nrows // step)
                def _(m):
                    at = pl.ds(pl.multiple_of(m * step, step), step)
                    acc = lax.dot_general(left[owner, at, :], both[...], NT, preferred_element_type=F32)
                    acc += lax.dot_general(left[owner, at, :width], low[...], NT, preferred_element_type=F32)
                    out[where, at, :] += acc


def multiply(jobs, sources, band, scal, ready, before, height, width):
    nrows = ready[0].shape[1]
    piece = jax.ShapeDtypeStruct((2, nrows, height), F32)
    inputs = (scal,) + tuple(ready) + tuple(before) + tuple(sources)
    return pl.pallas_call(
        functools.partial(multiply_kernel, jobs, band, not before),
        out_shape=(piece, piece),
        in_specs=[SMEM] + [VMEM] * (2 + len(before)) + [ANY] * len(sources),
        out_specs=[VMEM, VMEM],
        scratch_shapes=[
            pltpu.VMEM((len(jobs), height, width), F32),
            pltpu.VMEM((height, 2 * width), BF16),
            pltpu.VMEM((height, width), BF16),
            pltpu.SemaphoreType.DMA((len(jobs),)),
        ],
        input_output_aliases={3: 0, 4: 1} if before else {},
        compiler_params=pltpu.CompilerParams(vmem_limit_bytes=36 << 20),
        cost_estimate=pl.CostEstimate(
            flops=12 * nrows * height * width * max(1, len(jobs) // 2), bytes_accessed=16 << 20, transcendentals=0
        ),
        name="multiply_%d_%d" % (band, len(jobs)),
    )(*inputs)


def finish_kernel(scal, left, right, *refs):
    refs[-1][...] = left[0] + right[0]


def finish(scal, band, mine, received, before, hours):
    pieces, nrows, height = mine.shape
    half = nrows // 2
    from_acc = pl.BlockSpec((1, half, height), lambda i, r, s: (r, i, 0))

    def place(i, r, s):
        return (jnp.where(s[3] == 0, 1 - i, i), pieces * band + r)

    return pl.pallas_call(
        finish_kernel,
        out_shape=jax.ShapeDtypeStruct((nrows, hours), F32),
        grid_spec=pltpu.PrefetchScalarGridSpec(
            num_scalar_prefetch=1,
            grid=(2, pieces),
            in_specs=[from_acc, from_acc] + [ANY] * len(before),
            out_specs=pl.BlockSpec((half, height), place),
        ),
        input_output_aliases={3: 0} if before else {},
        compiler_params=pltpu.CompilerParams(vmem_limit_bytes=16 << 20),
        cost_estimate=pl.CostEstimate(
            flops=nrows * height * pieces, bytes_accessed=12 * nrows * height * pieces, transcendentals=0
        ),
        name="finish_%d" % band,
    )(scal, mine, received, *before)


def paired(noise, factor, col_blocks, block_values):
    node_rows, hours = noise.shape
    height, width = factor.shape[0] // 4, factor.shape[1]
    half = node_rows // 2
    space = lax.axis_size("space")
    chips = space // 2
    tm = lax.axis_size("tm")
    group, place, hour = lax.axis_index("groups"), lax.axis_index("space"), lax.axis_index("tm")
    chip, core = place // 2, place % 2
    blocks = node_rows // BS
    scal = jnp.stack([group, hour, chip, core, jnp.int32(chips), place * blocks, jnp.int32(space * blocks)])

    other_core = [(i, i ^ 1) for i in range(space)]
    across = [(i, (i + 1) % space) for i in range(1, space, 2)]
    across += [(target, source) for source, target in across]

    def device(z, c, x):
        return (2 * z + c) * tm + x

    def carried(band, x, z):
        return 2 * z * width < (4 * x + 2 * band + 2) * height

    def along(chunk, band, hop):
        sign = 1 if hop < 0 else -1
        route = []
        for z in range(chips):
            begin = z + hop + sign
            if 0 <= begin < chips and 0 <= z + sign < chips:
                route += [
                    (device(z, c, x), device(z + sign, c, x)) for c in range(2) for x in range(tm) if carried(band, x, begin)
                ]
        return lax.ppermute(chunk, ("space", "tm"), route) if route else None

    def swapped(chunk, band, hop):
        count = space * tm
        route = []
        for z in range(chips):
            if 0 <= z + hop < chips:
                for c in range(2):
                    for x in range(tm):
                        if carried(band, x, z + hop):
                            d = device(z, c, x)
                            route += [(d, count + d), (count + d, d)]
        return lax.ppermute(chunk, ("groups", "space", "tm"), route)

    mid = lax.dynamic_slice_in_dim(noise, half * (1 - core), half, 0)
    outer = lax.dynamic_slice_in_dim(noise, half * core, half, 0)
    far_mid = lax.ppermute(mid, "space", other_core)
    far_outer = lax.ppermute(outer, "space", across)

    received = {}
    moving = {}
    for band in (1, 0):
        chunk = lax.dynamic_slice_in_dim(factor, (2 * band + group) * height, height, 0)
        moving[band, 1], moving[band, -1] = chunk, chunk
    for distance in range(1, chips):
        for band in (1, 0):
            for sign in (1, -1):
                hop = -sign * distance
                chunk = along(moving[band, sign], band, hop)
                if chunk is not None:
                    moving[band, sign] = chunk
                    received[band, hop] = [chunk, swapped(chunk, band, hop)]

    ready = ()
    pieces = {}
    for outside, (side, far) in enumerate((("mid", far_mid), ("outer", far_outer))):
        keep, send = precision(side, scal, col_blocks, block_values, noise, far, width)
        theirs = lax.ppermute(send, "space", other_core)
        pieces[outside] = (keep, theirs)
        ready = prepare(scal, keep, theirs, outside, False, ready, width)
    for outside in range(2):
        later = [lax.ppermute(piece, "tm", [(0, 1)]) for piece in pieces[outside]]
        ready = prepare(scal, later[0], later[1], outside, True, ready, width)

    sums = {0: (), 1: ()}
    for distance in range(1, chips):
        for band in (1, 0):
            jobs, sources = [], []
            if distance == 1:
                sources.append(factor)
                jobs += [(0, 0, 0, "own"), (0, 1, 0, "own")]
            for hop in (-distance, distance):
                if (band, hop) in received:
                    for chunk, kind in zip(received[band, hop], ("direct", "swapped")):
                        jobs.append((len(sources), 0, hop, kind))
                        sources.append(chunk)
            sums[band] = multiply(jobs, sources, band, scal, ready, sums[band], height, width)
    out = ()
    for band in (1, 0):
        mine, theirs = sums[band]
        out = (finish(scal, band, mine, lax.ppermute(theirs, "space", other_core), out, 4 * height),)
    return out[0]


def fits(mesh):
    shape = mesh.shape
    return shape["groups"] == 2 and shape["tm"] == 2 and shape["rep"] == 1 and shape["space"] % 2 == 0 and shape["space"] >= 4


def per_device(mesh, noise, factor, col_blocks, block_values):
    rows, width = factor.shape
    nodes, hours = noise.shape
    square = fits(mesh) and nodes == 4 * BS and rows == 4 * width and hours == rows and rows * 2 == width * mesh.shape["space"]
    if square and width % 128 == 0 and REACH * BS * 2 == nodes:
        return paired(noise, factor, col_blocks, block_values)
    return general(noise, factor, col_blocks, block_values)


def solution(mesh):
    return jax.shard_map(
        functools.partial(per_device, mesh),
        mesh=mesh,
        in_specs=(
            P(("groups", "space"), "tm"),
            P(("tm", "rep"), "space"),
            P(("groups", "space"), None),
            P(("groups", "space"), None, None, None),
        ),
        out_specs=P(("groups", "space"), ("tm", "rep")),
        check_vma=False,
    )
```
